256 devices in a mesh: gy: 8 (over z), gx: 32 (over y, x, core).
Axes of the slice: x: 4, y: 4, z: 8, core: 2. Of those that a mesh axis runs over, the one named last changes fastest.
Arguments:
- positions: float32 [3, 32, 65536], P(None, 'gx', 'gy'), may hold values from -6 to 6
- velocities: float32 [3, 32, 65536], P(None, 'gx', 'gy'), may hold values from -6 to 6
- radius: float32 [32, 65536], P('gx', 'gy'), may hold values from 0.6 to 1
- sphere_cell: int32 [32, 65536], P('gx', 'gy'), may hold values from -1 to 16383, as said below
- pair_route: int32 [32, 512, 1], P('gx', 'gy'), may hold values from 0 to 30; in each aligned block of 64 rows (0 to 63, 64 to 127, ..., all dimensions but the last counted through in order) at most 4 rows name the same one
- pair_mine: int32 [32, 512], P('gx', 'gy'), may hold values from 0 to 63
- pair_theirs: int32 [32, 512], P('gx', 'gy'), may hold values from 0 to 63
- brick_owner: int32 [32, 8], P('gx'), may hold values from 0 to 7, each once within a row
- fluid_velocity: float32 [3, 32, 16384], P(None, 'gx', 'gy'), may hold values from -6 to 6
- pressure_grad: float32 [3, 32, 16384], P(None, 'gx', 'gy'), may hold values from -6 to 6
Outputs:
- new_velocity: float32 [3, 32, 65536], P(None, 'gx', 'gy')
- drag_source: float32 [3, 32, 16384], P(None, 'gx', 'gy')
The draws below stay inside these ranges and needn't reach their ends.
Inputs may be any that keep to these rules, and one draw needn't show every extreme that they name: `pair_route`: the pairs of one device name one offset at most 4 times, a bound that some block reaches. `sphere_cell`: in every block of 128 slots the live slots come first and are half of the block or more; every device has a full block.
All inputs are finite; a program needn't handle non-finite values.
Results may differ from the reference program's by a relative error of at most 0.0003.
Values sent between devices are 32-bit elements; how exact they have to be, the bound alone decides.
No kernel may reach another device: no remote copies, remote signals or barrier semaphores. Data moves between devices by JAX's collectives and lax.ppermute only.
A program may use at most 128 MiB of HBM per device.

```python
import math
import jax
import jax.numpy as jnp
import numpy as np
from jax import lax

BLOCK = 128
BLK_DEV = 64
CELLS_DEV = 2048
PAIRS_DEV = 64
CAP = 4
SPH_COL = 65536
PAIR_COL = 512
NCOL = 16384
N_GY = 8
N_GX = 32


def draw_sphere_cell(key, part):
    base = jax.random.fold_in(key, 11)
    first_key, second_key, third_key = jax.random.split(base, 3)
    live_count = jax.random.randint(first_key, (N_GX, N_GY, BLK_DEV), BLOCK // 2, BLOCK + 1)
    full_block = jax.random.randint(second_key, (N_GX, N_GY, 1), 0, BLK_DEV)
    live_count = jnp.where(jnp.arange(BLK_DEV)[None, None, :] == full_block, BLOCK, live_count)
    cells = jax.random.randint(third_key, (N_GX, N_GY, BLK_DEV, BLOCK), 0, NCOL)
    slots = jnp.arange(BLOCK)[None, None, None, :]
    result = jnp.where(slots < live_count[..., None], cells, -1)
    return result.reshape(N_GX, SPH_COL).astype(jnp.int32)


def set_ends(values, own_key, least, top_value):
    dims = values.shape
    spot = [jax.random.randint(jax.random.fold_in(own_key, axis), (), 0, dims[axis]) for axis in range(len(dims))]
    values = values.at[tuple(spot)].set(least)
    longest = dims.index(max(dims))
    spot[longest] = (spot[longest] + 1) % dims[longest]
    return values.at[tuple(spot)].set(top_value)


def steps_of(stream_key, extent, shards, low, largest):
    gain, own = 1.0, jax.random.fold_in(stream_key, 6)
    for axis_at, blocks in shards:
        heights = jnp.exp(jax.random.uniform(jax.random.fold_in(own, axis_at), (blocks,), jnp.float32, low / len(shards), largest / len(shards)))
        gain = gain * jnp.repeat(heights, extent[axis_at] // blocks).reshape([-1 if axis == axis_at else 1 for axis in range(len(extent))])
    return gain


def shared_out(stream_key, own, number, rows, amount, top, reach, skew):
    order = jax.random.permutation(stream_key, amount)
    heavy_load, ordinary = load_shares(amount, rows * top, reach, skew, True), load_shares(amount, rows * top, reach, skew, False)
    places = jnp.arange(amount)

    def named(sizes, offset_by):
        used = int((sizes > 0).sum())
        fixed = max(1, used // 4)
        moved = fixed + (places - fixed + offset_by * (used - fixed)) % max(1, amount - fixed)
        return jnp.zeros((amount,), jnp.int32).at[order[jnp.where(places < fixed, places, moved)]].set(jnp.asarray(sizes, jnp.int32))

    sizes = jnp.where(number % 4 == 0, named(heavy_load, number // 4), named(ordinary, number - number // 4 - 1))
    mixed = jax.random.permutation(jax.random.fold_in(own, 3), amount)
    giver, sink = mixed[0:amount // 2 * 2:2], mixed[1:amount // 2 * 2:2]
    margin = jnp.minimum(sizes[giver] - 1, reach - sizes[sink]) // 2
    margin = jnp.where((giver == order[0]) | (sink == order[0]) | (sizes[sink] == 0), 0, jnp.maximum(margin, 0))
    moved = jax.random.randint(jax.random.fold_in(own, 4), (amount // 2,), 0, 1 << 20) % (margin + 1)
    sizes = sizes.at[giver].add(-moved).at[sink].add(moved)
    labels = jnp.searchsorted(jnp.cumsum(sizes), jnp.arange(rows * top), side="right").astype(jnp.int32)
    grid = labels.reshape(top, rows).T
    grid = grid[jax.random.permutation(jax.random.fold_in(own, 1), rows)]
    offset_by = jax.random.randint(jax.random.fold_in(own, 2), (rows, 1), 0, top)
    return jnp.take_along_axis(grid, (jnp.arange(top)[None, :] + offset_by) % top, axis=1)


def load_shares(count, total, most, lean, full):
    portions = [(1 << 20) // math.isqrt(standing ** lean) + 1 for standing in range(1, count + 1)]
    largest = most if full else min(most, max(-(-total // count), total * portions[0] // sum(portions)))
    least = 1 if total - largest >= count - 1 else 0
    given, rest = [largest] + [least] * (count - 1), total - largest - least * (count - 1)
    while rest > 0:
        candidates = [i for i in range(1, count) if given[i] < largest] or [i for i in range(1, count) if given[i] < most]
        whole, remaining = sum([portions[i] for i in candidates]), rest
        for i in candidates:
            more = min(most - given[i], max(1, remaining * portions[i] // whole), rest)
            given[i] = given[i] + more
            rest = rest - more
    return np.array(given)


def noise(rng, shape, deviation, limit, cuts=(), kind=jnp.bfloat16):
    values = jax.random.normal(rng, shape, jnp.float32) * deviation
    if len(cuts) > 0:
        values = steps_of(rng, shape, cuts, -0.22, 0.18) * values
    return jnp.clip(values, min=-limit, max=limit).astype(kind)


def setup_inputs(seed: int = 0) -> dict:
    splits = jax.random.split(jax.random.key(seed), 11)
    positions = noise(splits[0], (3, N_GX, SPH_COL), 1.0, 6.0, ((1, 32), (2, 8)), jnp.float32)
    velocities = noise(splits[1], (3, N_GX, SPH_COL), 1.0, 6.0, ((1, 32), (2, 8)), jnp.float32)
    radius = jnp.clip(jnp.exp(math.log(1.0) - 0.5108256 * jax.random.uniform(splits[2], (N_GX, SPH_COL), jnp.float32) ** steps_of(splits[2], (N_GX, SPH_COL), ((0, 32), (1, 8)), -0.2, 0.2)), 0.6, 1.0)
    sphere_cell = draw_sphere_cell(jax.random.fold_in(splits[10], 71), 0)
    pair_route_keys = jax.random.split(jax.random.fold_in(splits[4], 1), N_GX * PAIR_COL // PAIRS_DEV)
    pair_route_turns = jax.random.permutation(jax.random.fold_in(splits[4], 3), N_GX * PAIR_COL // PAIRS_DEV)
    pair_route = jax.vmap(lambda own, number: shared_out(jax.random.fold_in(splits[4], 2), own, number, PAIRS_DEV, N_GX - 1, 1, CAP, 2))(pair_route_keys, pair_route_turns).reshape((N_GX, PAIR_COL, 1))
    pair_mine = set_ends(jax.random.randint(splits[5], (N_GX, PAIR_COL), 0, BLK_DEV), jax.random.fold_in(splits[5], 1), 0, BLK_DEV - 1).astype(jnp.int32)
    pair_theirs = set_ends(jax.random.randint(splits[6], (N_GX, PAIR_COL), 0, BLK_DEV), jax.random.fold_in(splits[6], 1), 0, BLK_DEV - 1).astype(jnp.int32)
    brick_owner = jax.vmap(lambda own: jax.random.permutation(own, N_GY))(jax.random.split(splits[7], N_GX)).reshape((N_GX, N_GY)).astype(jnp.int32)
    fluid_velocity = noise(splits[8], (3, N_GX, NCOL), 1.0, 6.0, ((1, 32), (2, 8)), jnp.float32)
    pressure_grad = noise(splits[9], (3, N_GX, NCOL), 1.0, 6.0, ((1, 32), (2, 8)), jnp.float32)
    return dict(positions=positions, velocities=velocities, radius=radius, sphere_cell=sphere_cell, pair_route=pair_route, pair_mine=pair_mine, pair_theirs=pair_theirs, brick_owner=brick_owner, fluid_velocity=fluid_velocity, pressure_grad=pressure_grad)


stiffness = 0.05
damping = 0.02
drag_coeff = 0.5
time_step = 0.2


def contact(left_state, right_state):
    offset = left_state[:, 0:3, :, None] - right_state[:, 0:3, None, :]
    dist_sq = offset[:, 0] * offset[:, 0] + offset[:, 1] * offset[:, 1] + offset[:, 2] * offset[:, 2]
    radius_sum = left_state[:, 6, :, None] + right_state[:, 6, None, :]
    weight = jnp.exp(-dist_sq / (2.0 * radius_sum * radius_sum)) * (left_state[:, 7, :, None] * right_state[:, 7, None, :])
    relative = left_state[:, 3:6, :, None] - right_state[:, 3:6, None, :]
    pulling = weight[:, None] * (stiffness * offset - damping * relative)
    return jnp.sum(pulling, axis=3), -jnp.sum(pulling, axis=2)


def contact_pair(pair_in):
    return contact(pair_in[0], pair_in[1])


def grouped(left_all, right_all):
    count_all = left_all.shape[0]
    group_size = math.gcd(count_all, 8)
    shaped = (left_all.reshape(count_all // group_size, group_size, 8, BLOCK),
              right_all.reshape(count_all // group_size, group_size, 8, BLOCK))
    on_left, on_right = lax.map(contact_pair, shaped)
    return on_left.reshape(count_all, 3, BLOCK), on_right.reshape(count_all, 3, BLOCK)


def reference(positions, velocities, radius, sphere_cell, pair_route, pair_mine, pair_theirs, brick_owner, fluid_velocity, pressure_grad):
    alive_mask = (sphere_cell >= 0).astype(jnp.float32)
    states = jnp.concatenate([positions, velocities, radius[None], alive_mask[None]], axis=0)
    states = states.reshape(8, N_GX, N_GY, BLK_DEV, BLOCK).transpose(1, 2, 3, 0, 4)

    def one_device(forces, flat_index):
        column = (flat_index // N_GY).astype(jnp.int32)
        row_index = (flat_index % N_GY).astype(jnp.int32)
        own_blocks = states[column, row_index]
        beside = jnp.concatenate([own_blocks[1:], jnp.zeros_like(own_blocks[:1])], axis=0)
        self_force, unused_self = grouped(own_blocks, own_blocks)
        near_force, back_force = grouped(own_blocks, beside)
        local_force = self_force + near_force + jnp.concatenate([jnp.zeros_like(back_force[:1]), back_force[:-1]], axis=0)
        start_at = (row_index * PAIRS_DEV).astype(jnp.int32)
        route_off = lax.dynamic_slice_in_dim(pair_route[column, :, 0], start_at, PAIRS_DEV)
        mine_index = lax.dynamic_slice_in_dim(pair_mine[column], start_at, PAIRS_DEV)
        theirs = lax.dynamic_slice_in_dim(pair_theirs[column], start_at, PAIRS_DEV)
        target = ((column + 1 + route_off) % N_GX).astype(jnp.int32)
        partner = states[target, row_index, theirs]
        on_owner, on_partner = grouped(own_blocks[mine_index], partner)
        forces = forces.at[column, row_index].add(local_force)
        forces = forces.at[column, row_index, mine_index].add(on_owner)
        forces = forces.at[target, row_index, theirs].add(on_partner)
        return forces, None

    start_forces = jnp.zeros((N_GX, N_GY, BLK_DEV, 3, BLOCK), jnp.float32)
    forces, unused_out = lax.scan(one_device, start_forces, jnp.arange(N_GX * N_GY, dtype=jnp.int32))
    contact_force = forces.transpose(3, 0, 1, 2, 4).reshape(3, N_GX, SPH_COL)

    block_of = jnp.clip(sphere_cell // CELLS_DEV, 0, N_GY - 1).astype(jnp.int32)
    within = sphere_cell % CELLS_DEV
    owner_of = jnp.take_along_axis(brick_owner, block_of, axis=1)
    storage = jnp.where(sphere_cell >= 0, owner_of * CELLS_DEV + within, 0).astype(jnp.int32)
    fluid_at = jnp.take_along_axis(fluid_velocity, storage[None], axis=2)
    grad_at = jnp.take_along_axis(pressure_grad, storage[None], axis=2)
    sphere_cube = radius * radius * radius
    drag_force = alive_mask * drag_coeff * radius * (fluid_at - velocities)
    fluid_force = drag_force - alive_mask * sphere_cube * grad_at
    new_velocity = velocities + time_step * (contact_force + fluid_force) / sphere_cube
    flat_cell = (jnp.arange(N_GX, dtype=jnp.int32)[:, None] * NCOL + storage).reshape(-1)
    deposit = jax.ops.segment_sum(-drag_force.reshape(3, -1).T, flat_cell, num_segments=N_GX * NCOL)
    drag_source = deposit.T.reshape(3, N_GX, NCOL)
    return new_velocity, drag_source
```

```python
import functools

import jax
import jax.numpy as jnp
from jax import lax
from jax.experimental import pallas as pl
from jax.experimental.pallas import tpu as pltpu
from jax.sharding import PartitionSpec as P


stiffness = 0.05
damping = 0.02
drag_coeff = 0.5
time_step = 0.2

LANES = 128
CAP = 4
UNROLL = 4
CHUNK = 4
WIDE = 2
SPLIT = 256
HALF_LOG2E = 0.7213475204444817
F32 = jnp.float32
BF16 = jnp.bfloat16

VMEM_SPEC = pl.BlockSpec(memory_space=pltpu.VMEM)
RAW_SPEC = pl.BlockSpec(memory_space=pl.ANY)
SMEM_SPEC = pl.BlockSpec(memory_space=pltpu.SMEM)


def pieces(value, count):
    found = []
    rest = value
    for step in range(count):
        part = rest.astype(BF16).astype(F32)
        found.append(part)
        if step + 1 < count:
            rest = rest - part
    return found


def row_ids(shape):
    return lax.broadcasted_iota(jnp.int32, shape, 0)


def prep_kernel(gx_count, route, mine, theirs, pos, vel, rad, cell, push, slots, state, used):
    me = lax.axis_index("gx")
    blocks = rad.shape[0]
    for c in range(3):
        state[0:blocks, c, :] = stiffness * pos[c] - damping * vel[c]
        state[0:blocks, 4 + c, :] = pos[c]
    state[0:blocks, 3, :] = (cell[...] >= 0).astype(F32)
    state[0:blocks, 7, :] = rad[...]
    state[blocks] = jnp.zeros((8, LANES), F32)
    push[...] = jnp.zeros(push.shape, F32)

    def clear(t, carry):
        used[t] = 0
        return carry

    lax.fori_loop(0, gx_count, clear, 0, unroll=8)
    tag = (row_ids((8, LANES)) == 3) & (lax.broadcasted_iota(jnp.int32, (8, LANES), 1) == 0)

    def place(p, carry):
        dest = lax.rem(me + 1 + route[p], gx_count)
        order = used[dest]
        used[dest] = order + 1
        slot = dest * CAP + order
        slots[p] = slot
        label = (theirs[p] + 1).astype(F32)
        push[slot] = jnp.where(tag, label, state[mine[p]])
        return carry

    lax.fori_loop(0, route.shape[0], place, 0, unroll=4)


def split_state(tile):
    rows = row_ids(tile.shape)
    scaled = jnp.where(rows < 4, 0.0, jnp.where(rows < 7, tile * (HALF_LOG2E**0.5), tile))
    square = scaled * scaled
    dist = jnp.sum(jnp.where(rows < 7, square, 0.0), axis=0, keepdims=True)
    size = jnp.sum(jnp.where(rows == 7, square, 0.0), axis=0, keepdims=True)
    return rows, scaled, dist, size


def norm_tile(rows, at, value, other):
    first, second, third = pieces(value, 3)
    inner = jnp.where(rows == at, first, jnp.where(rows == at + 1, second, third))
    here = (rows >= at) & (rows < at + 3)
    return jnp.where(here, inner, jnp.where(rows < 6, other, 0.0))


def right_features(tile):
    rows, scaled, dist, size = split_state(tile)
    high, mid, low = pieces(scaled, 3)
    tiles = [high, mid, high, mid, low, high]
    tiles.append(norm_tile(rows, 3, dist, 1.0))
    tiles.append(norm_tile(rows, 3, size, 1.0))
    return jnp.concatenate(tiles, axis=0).astype(BF16)


def left_features(tile):
    rows, scaled, dist, size = split_state(tile)
    high, mid, low = pieces(2.0 * scaled, 3)
    tiles = [high, high, mid, mid, high, low]
    tiles.append(norm_tile(rows, 0, -dist, -1.0))
    tiles.append(norm_tile(rows, 0, size, 1.0))
    return jnp.concatenate(tiles, axis=0).T.astype(BF16)


def left_pair(features):
    lane = lax.broadcasted_iota(jnp.int32, features.shape, 1)
    to_dist = ((lane < 48) & (lane % 8 != 7)) | ((lane >= 48) & (lane < 56))
    zero = jnp.zeros_like(features)
    return jnp.concatenate(
        [jnp.where(to_dist, zero, features), jnp.where(to_dist, features, zero)], axis=0
    )


def sums(tile):
    rows = row_ids(tile.shape)
    kept = jnp.where(rows < 4, tile * tile[3:4], 0.0)
    high, mid, low = pieces(kept, 3)
    return jnp.concatenate([high, mid, low, jnp.zeros_like(high)], axis=0).astype(BF16)


def weigh(pair, weight):
    size, dist = pair[0:LANES], pair[LANES : 2 * LANES]
    inverse = pl.reciprocal(size, approx=True)
    value = jnp.exp2((dist * inverse) * (2.0 - size * inverse))
    high = value.astype(BF16)
    weight[0] = high
    weight[1] = (value - high.astype(F32)).astype(BF16)


def over_right(summed, weight):
    dims = (((1,), (1,)), ((), ()))
    return lax.dot_general(summed, weight[0], dims, preferred_element_type=F32) + lax.dot_general(
        summed, weight[1], dims, preferred_element_type=F32
    )


def over_left(summed, high, low):
    return jnp.dot(summed, high, preferred_element_type=F32) + jnp.dot(
        summed, low, preferred_element_type=F32
    )


def pull(tile, product):
    total = product[0:8] + product[8:16] + product[16:24]
    return tile[3:4] * (tile * total[3:4] - total)


def local_kernel(state, ahead, force, features, summed, right, pair, weight):
    del ahead
    blocks = features.shape[0]
    force[...] = jnp.zeros(force.shape, F32)
    weight[...] = jnp.zeros(weight.shape, BF16)
    pair[...] = jnp.ones(pair.shape, F32)

    def prepare(b, carry):
        tile = state[b]
        features[b] = left_features(tile)
        right[b] = right_features(tile)
        summed[b] = sums(tile)
        return carry

    lax.fori_loop(0, blocks, prepare, 0, unroll=4)
    right[blocks] = right_features(state[blocks])
    summed[blocks] = sums(state[blocks])

    def turn(i, now):
        live = i >= 2
        ends = []
        for k in range(WIDE):
            done = jnp.maximum(WIDE * (i - 2) + k, 0)
            held = weight.at[now, k]
            on_here = over_right(jnp.concatenate([summed[done], summed[done + 1]], axis=1), held)
            on_beside = over_left(summed[done], held[0, :, LANES:], held[1, :, LANES:])
            ends.append((done, on_here, on_beside))
        for k in range(WIDE):
            weigh(pair.at[1 - now, k], weight.at[1 - now, k])
        for k in range(WIDE):
            b = jnp.minimum(WIDE * i + k, blocks - 1)
            pair[now, k] = jnp.dot(
                left_pair(features[b]),
                jnp.concatenate([right[b], right[b + 1]], axis=1),
                preferred_element_type=F32,
            )
        for done, on_here, on_beside in ends:
            force[done] = force[done] + jnp.where(live, pull(state[done], on_here), 0.0)
            force[done + 1] = force[done + 1] + jnp.where(live, pull(state[done + 1], on_beside), 0.0)

    def step(i, carry):
        turn(2 * i, 0)
        turn(2 * i + 1, 1)
        return carry

    lax.fori_loop(0, (blocks // WIDE + 2) // 2, step, 0)


def label_kernel(came, listed, total, tags, sem):
    slot_total = came.shape[0]
    fetch = pltpu.make_async_copy(came.at[:, 3, :], tags, sem)
    fetch.start()
    fetch.wait()

    def pick(s, count):
        block = tags[s, 0].astype(jnp.int32) - 1
        listed[count, 0] = s
        listed[count, 1] = jnp.maximum(block, 0)
        return count + jnp.where(block >= 0, 1, 0)

    count = lax.fori_loop(0, slot_total, pick, 0, unroll=8)
    spare = lax.axis_index("gx") * CAP
    for extra in range(UNROLL):
        listed[count + extra, 0] = spare
        listed[count + extra, 1] = 0
    total[0] = count


def remote_kernel(
    listed, total, state, features, summed, force_in, came, force, back, right, others, tiles, pair, weight
):
    force[...] = force_in[...]
    weight[...] = jnp.zeros(weight.shape, BF16)
    pair[...] = jnp.ones(pair.shape, F32)
    rows = row_ids((8, LANES))
    tag = (rows == 3) & (lax.broadcasted_iota(jnp.int32, (8, LANES), 1) == 0)
    count = total[0]

    def prepare(i, carry):
        for u in range(UNROLL):
            at = i * UNROLL + u
            raw = came[listed[at, 0]]
            tile = jnp.where(tag, jnp.minimum(raw, 1.0), raw)
            tiles[at] = tile
            right[at] = right_features(tile)
            others[at] = sums(tile)
        return carry

    groups = (count + UNROLL) // UNROLL
    last = UNROLL * groups - 1
    lax.fori_loop(0, groups, prepare, 0)

    def turn(i, now):
        live = i >= 2
        ends = []
        for k in range(WIDE):
            done = jnp.clip(WIDE * (i - 2) + k, 0, last)
            block = listed[done, 1]
            held = weight.at[now, k]
            on_own = over_right(others[done], held)
            on_other = over_left(summed[block], held[0], held[1])
            ends.append((done, block, on_own, on_other))
        for k in range(WIDE):
            weigh(pair.at[1 - now, k], weight.at[1 - now, k])
        for k in range(WIDE):
            at = jnp.minimum(WIDE * i + k, last)
            pair[now, k] = jnp.dot(
                left_pair(features[listed[at, 1]]), right[at], preferred_element_type=F32
            )
        for done, block, on_own, on_other in ends:
            force[block] = force[block] + jnp.where(live, pull(state[block], on_own), 0.0)
            back[listed[done, 0]] = pull(tiles[done], on_other)[0:4]

    def step(i, carry):
        turn(2 * i, 0)
        turn(2 * i + 1, 1)
        return carry

    lax.fori_loop(0, groups + 1, step, 0)


def scatter_kernel(
    cells_dev, owner, cell, vel, rad, speed, slope, after, out, columns, lines, copies, acc, split, left, right
):
    del after
    for g in range(copies.shape[0]):
        for c in range(3):
            copies[g, c] = speed[c]
            copies[g, 3 + c] = slope[c]
    here = cell[...]
    brick = here // cells_dev
    stored = jnp.zeros_like(here)
    for j in range(owner.shape[0]):
        stored = jnp.where(brick == j, owner[j], stored)
    stored = jnp.where(here >= 0, stored * cells_dev + (here & (cells_dev - 1)), 0)
    columns[...] = (stored & 127) + ((stored >> 13) << 7)
    lines[...] = (stored >> 7) & 63
    amount = jnp.where(here >= 0, drag_coeff * rad[...], 0.0)
    for c in range(4):
        high, low = pieces(amount if c == 0 else amount * vel[c - 1], 2)
        split[2 * c] = high
        split[2 * c + 1] = low
    acc[...] = jnp.zeros(acc.shape, F32)
    chunk = left.shape[2] // LANES
    chunks = cell.shape[0] // chunk

    def build(t, buf):
        fine = row_ids((SPLIT, LANES))
        coarse = row_ids((64, LANES))
        for u in range(chunk):
            at = pl.ds(t * chunk + u, 1)
            lo = u * LANES
            right[buf, :, lo : lo + LANES] = jnp.where(fine == columns[at, :], 1.0, 0.0).astype(BF16)
            mask = coarse == lines[at, :]
            for p in range(8):
                left[buf, 64 * p : 64 * p + 64, lo : lo + LANES] = jnp.where(
                    mask, split[p, at, :], 0.0
                ).astype(BF16)

    build(0, 0)

    def step(i, carry):
        for now in range(2):
            t = 2 * i + now
            acc[...] += lax.dot_general(
                left[now], right[now], (((1,), (1,)), ((), ())), preferred_element_type=F32
            )
            build(jnp.minimum(t + 1, chunks - 1), 1 - now)
        return carry

    lax.fori_loop(0, chunks // 2, step, 0)
    for g in range(out.shape[0]):
        for c in range(4):
            lo = (g // 4) * LANES
            at = c * 128 + (g % 4) * 16
            out[g, c] = acc[at : at + 16, lo : lo + LANES] + acc[at + 64 : at + 80, lo : lo + LANES]


def gather_kernel(columns, lines, cell, vel, rad, table, parts, speed, fluid, out, wide, picked, found):
    whole = [sum(parts[g, c] for g in range(parts.shape[0])) for c in range(4)]
    for c in range(3):
        out[c] = whole[1 + c] - speed[c] * whole[0]
    for owner in range(table.shape[0]):
        high, low = pieces(table[owner].reshape(96, LANES), 2)
        wide[0, owner // 4, owner % 4] = high.astype(BF16)
        wide[1, owner // 4, owner % 4] = low.astype(BF16)
    chunks = cell.shape[0] // 2

    def look(t, buf):
        fine = row_ids((SPLIT, LANES))
        hot = jnp.concatenate(
            [
                jnp.where(fine == columns[pl.ds(2 * t + u, 1), :], 1.0, 0.0).astype(BF16)
                for u in range(2)
            ],
            axis=1,
        )
        total = None
        for p in range(2):
            side = jnp.concatenate([wide[p, half].reshape(384, LANES) for half in range(2)], axis=1)
            term = jnp.dot(side, hot, preferred_element_type=F32)
            total = term if total is None else total + term
        picked[buf] = total

    look(0, 0)

    def step(i, carry):
        for now in range(2):
            t = 2 * i + now
            coarse = row_ids((64, LANES))
            for u in range(2):
                at = pl.ds(2 * t + u, 1)
                lo = u * LANES
                mask = coarse == lines[at, :]
                for c in range(6):
                    total = None
                    for q in range(4):
                        row = q * 96 + c * 16
                        term = jnp.where(
                            mask[q * 16 : q * 16 + 16], picked[now, row : row + 16, lo : lo + LANES], 0.0
                        )
                        total = term if total is None else total + term
                    found[c, at, :] = jnp.sum(total, axis=0, keepdims=True)
            look(jnp.minimum(t + 1, chunks - 1), 1 - now)
        return carry

    lax.fori_loop(0, chunks // 2, step, 0)
    size = rad[...]
    live = (cell[...] >= 0).astype(F32)
    cube = size * size * size
    for c in range(3):
        drag = live * drag_coeff * size * (found[c] - vel[c])
        fluid[c] = drag - live * cube * found[3 + c]


def final_kernel(slots, mine, force, back, fluid, vel, rad, out, total):
    blocks = rad.shape[0]
    total[...] = force[0:blocks]

    def add(p, carry):
        block = mine[p]
        total[block, 0:4] = total[block, 0:4] + back[slots[p]]
        return carry

    lax.fori_loop(0, mine.shape[0], add, 0, unroll=4)
    size = rad[...]
    cube = size * size * size
    for c in range(3):
        out[c] = vel[c] + time_step * (total[:, c, :] + fluid[c]) / cube


def call(body, outs, args, smem=(), smem_out=(), raw=(), raw_out=(), scratch=(), alias=None, flops=0):
    return pl.pallas_call(
        body,
        out_shape=[jax.ShapeDtypeStruct(s, d) for s, d in outs],
        in_specs=[SMEM_SPEC if i in smem else RAW_SPEC if i in raw else VMEM_SPEC for i in range(len(args))],
        out_specs=[
            SMEM_SPEC if i in smem_out else RAW_SPEC if i in raw_out else VMEM_SPEC
            for i in range(len(outs))
        ],
        scratch_shapes=list(scratch),
        input_output_aliases=alias or {},
        cost_estimate=pl.CostEstimate(flops=flops, bytes_accessed=1 << 20, transcendentals=0),
    )(*args)


def on_device(
    positions,
    velocities,
    radius,
    sphere_cell,
    pair_route,
    pair_mine,
    pair_theirs,
    brick_owner,
    fluid_velocity,
    pressure_grad,
):
    gx_count, gy_count = lax.axis_size("gx"), lax.axis_size("gy")
    blocks = positions.shape[2] // LANES
    cells_dev = fluid_velocity.shape[2]
    cell_rows = cells_dev // LANES
    pairs = pair_mine.shape[1]
    slot_total = gx_count * CAP
    pos = positions.reshape(3, blocks, LANES)
    vel = velocities.reshape(3, blocks, LANES)
    rad = radius.reshape(blocks, LANES)
    cell = sphere_cell.reshape(blocks, LANES)
    speed = fluid_velocity.reshape(3, cell_rows, LANES)
    slope = pressure_grad.reshape(3, cell_rows, LANES)
    route, mine, theirs = pair_route.reshape(pairs), pair_mine.reshape(pairs), pair_theirs.reshape(pairs)

    push, slots, state = call(
        functools.partial(prep_kernel, gx_count),
        [((slot_total, 8, LANES), F32), ((pairs,), jnp.int32), ((blocks + 1, 8, LANES), F32)],
        (route, mine, theirs, pos, vel, rad, cell),
        smem=(0, 1, 2),
        smem_out=(1,),
        scratch=[pltpu.SMEM((gx_count,), jnp.int32)],
    )
    came = exchange(push.reshape(gx_count, CAP * 8, LANES), "gx")
    came = came.reshape(slot_total, 8, LANES)

    parts, columns, lines, copies = call(
        functools.partial(scatter_kernel, cells_dev),
        [
            ((gy_count, 4, cell_rows, LANES), F32),
            ((blocks, LANES), jnp.int32),
            ((blocks, LANES), jnp.int32),
            ((gy_count, 6, cell_rows, LANES), F32),
        ],
        (brick_owner.reshape(-1), cell, vel, rad, speed, slope, slots),
        smem=(0, 6),
        scratch=[
            pltpu.VMEM((512, SPLIT), F32),
            pltpu.VMEM((8, blocks, LANES), F32),
            pltpu.VMEM((2, 512, CHUNK * LANES), BF16),
            pltpu.VMEM((2, SPLIT, CHUNK * LANES), BF16),
        ],
        flops=2 * 10**9,
    )
    listed, total = call(
        label_kernel,
        [((slot_total + UNROLL, 2), jnp.int32), ((1,), jnp.int32)],
        (came,),
        smem_out=(0, 1),
        raw=(0,),
        scratch=[pltpu.SMEM((slot_total, LANES), F32), pltpu.SemaphoreType.DMA],
    )
    force, features, summed = call(
        local_kernel,
        [
            ((blocks + 1, 8, LANES), F32),
            ((blocks, LANES, 64), BF16),
            ((blocks + 1, 32, LANES), BF16),
        ],
        (state, total),
        flops=4 * 10**9,
        raw=(1,),
        scratch=[
            pltpu.VMEM((blocks + 1, 64, LANES), BF16),
            pltpu.VMEM((2, WIDE, 2 * LANES, 2 * LANES), F32),
            pltpu.VMEM((2, WIDE, 2, LANES, 2 * LANES), BF16),
        ],
    )
    table = exchange(copies.reshape(gy_count, 6 * cell_rows, LANES), "gy")
    table = table.reshape(gy_count, 6, cell_rows, LANES)
    parts = exchange(parts.reshape(gy_count, 4 * cell_rows, LANES), "gy")
    parts = parts.reshape(gy_count, 4, cell_rows, LANES)

    room = slot_total + UNROLL
    force, back = call(
        remote_kernel,
        [((blocks + 1, 8, LANES), F32), ((slot_total, 4, LANES), F32)],
        (listed, total, state, features, summed, force, came),
        smem=(0, 1),
        scratch=[
            pltpu.VMEM((room, 64, LANES), BF16),
            pltpu.VMEM((room, 32, LANES), BF16),
            pltpu.VMEM((room, 8, LANES), F32),
            pltpu.VMEM((2, WIDE, 2 * LANES, LANES), F32),
            pltpu.VMEM((2, WIDE, 2, LANES, LANES), BF16),
        ],
        alias={5: 0},
        flops=4 * 10**9,
    )
    back = exchange(back.reshape(gx_count, CAP * 4, LANES), "gx")
    back = back.reshape(slot_total, 4, LANES)

    fluid, drag_source = call(
        gather_kernel,
        [((3, blocks, LANES), F32), ((3, cell_rows, LANES), F32)],
        (columns, lines, cell, vel, rad, table, parts, speed),
        scratch=[
            pltpu.VMEM((2, 2, 4, 96, LANES), BF16),
            pltpu.VMEM((2, 384, 2 * LANES), F32),
            pltpu.VMEM((6, blocks, LANES), F32),
        ],
        flops=3 * 10**9,
    )
    (new_velocity,) = call(
        final_kernel,
        [((3, blocks, LANES), F32)],
        (slots, mine, force, back, fluid, vel, rad),
        smem=(0, 1),
        scratch=[pltpu.VMEM((blocks, 8, LANES), F32)],
    )
    return new_velocity.reshape(3, 1, blocks * LANES), drag_source.reshape(3, 1, cells_dev)


def exchange(value, axis):
    return lax.all_to_all(value, axis, 0, 0, tiled=True)


def solution(mesh):
    placed = (
        P(None, "gx", "gy"),
        P(None, "gx", "gy"),
        P("gx", "gy"),
        P("gx", "gy"),
        P("gx", "gy", None),
        P("gx", "gy"),
        P("gx", "gy"),
        P("gx", None),
        P(None, "gx", "gy"),
        P(None, "gx", "gy"),
    )
    return jax.shard_map(
        on_device,
        mesh=mesh,
        in_specs=placed,
        out_specs=(P(None, "gx", "gy"), P(None, "gx", "gy")),
        check_vma=False,
    )
```
